32 devices in a mesh: groups: 2 (over y), tm: 16 (over z, x, core).
Axes of the slice: x: 2, y: 2, z: 4, core: 2. Of those that a mesh axis runs over, the one named last changes fastest.
Arguments:
- voltages: bfloat16 [256, 256, 2, 188], P(None, ('groups', 'tm')), parts along dimension 1, as said below
- off_starts: int32 [16], P('groups'), parts along dimension 0, may hold values from 0 to 124, as said below
- pointing: int32 [36], replicated, may hold values from 0 to 2047, as said below
- patterns: bfloat16 [2, 188, 2048], P(None, None, 'tm'), may hold values from -0.3125 to 0.3125
Outputs:
- beam_weights: bfloat16 [512, 2, 6768], P(('groups', 'tm')), parts along dimension 0
- beam_maps: float32 [512, 36, 2048], P('groups', None, 'tm'), parts along dimension 0
The draws below stay inside these ranges and needn't reach their ends.
There are 2 independent parts, one for each index of `groups`. The reference program is written for one: setup_inputs(seed, part) draws one part's arguments, and reference() takes and returns one part's arrays. A program takes and returns all parts, laid end to end along the dimension named above; an argument that names none is the same for every part. Nothing has to cross between parts.
Inputs may be any that keep to these rules, and one draw needn't show every extreme that they name: Complex port voltages: thermal noise whose power differs between ports and grows along time, plus sky signals common to the ports. `off_starts`: each of the 8 off-source ranges covers 4 samples from this start; ranges may intersect. `pointing`: several beams may point at the same pixel.
All inputs are finite; a program needn't handle non-finite values.
Results may differ from the reference program's by a relative error of at most 0.0034.
Values may be sent and summed in bfloat16 or wider, within the bound.
No kernel may reach another device: no remote copies, remote signals or barrier semaphores. Data moves between devices by JAX's collectives and lax.ppermute only.
A program may use at most 64 MiB of HBM per device.

```python
import math
import jax
import jax.numpy as jnp
from jax import lax

P_SIZE = 188
B = 36
CH = 256
ITERS = 20
RANGES = 8
TIME = 128
PIX = 2048
OFF_LEN = 4


def draw_voltages(key, part):
    subkeys = jax.random.split(jax.random.fold_in(key, 11), 4)
    thermal = jax.random.truncated_normal(subkeys[0], -5.0, 5.0, (CH, TIME, 2, P_SIZE), jnp.float32)
    port_amp = jnp.exp(jax.random.uniform(subkeys[1], (CH, 1, 1, P_SIZE), jnp.float32, 0.0, math.log(3.0)))
    gain_scale = 0.25
    drift = jnp.sqrt(1.0 + 2.0 * jnp.arange(TIME, dtype=jnp.float32) / TIME)
    sources = jax.random.normal(subkeys[2], (CH, TIME, 2, 3), jnp.float32)
    port_gains = gain_scale * jax.random.normal(subkeys[3], (CH, 3, 2, P_SIZE), jnp.float32)
    signal_real = jnp.einsum('ctk,ckp->ctp', sources[:, :, 0], port_gains[:, :, 0]) - jnp.einsum('ctk,ckp->ctp', sources[:, :, 1], port_gains[:, :, 1])
    signal_imag = jnp.einsum('ctk,ckp->ctp', sources[:, :, 0], port_gains[:, :, 1]) + jnp.einsum('ctk,ckp->ctp', sources[:, :, 1], port_gains[:, :, 0])
    return (thermal * port_amp * drift[None, :, None, None] + jnp.stack([signal_real, signal_imag], axis=2)).astype(jnp.bfloat16)


def draw_off_starts(key, part):
    drawn = jax.random.randint(jax.random.fold_in(key, 23), (RANGES,), 0, TIME - OFF_LEN + 1, dtype=jnp.int32)
    ranks = jnp.arange(RANGES, dtype=jnp.int32)
    return jnp.where(ranks == 0, 0, jnp.where(ranks == 1, TIME - OFF_LEN, drawn)).astype(jnp.int32)


def draw_pointing(key, part):
    drawn = jax.random.randint(jax.random.fold_in(key, 37), (B,), 0, PIX, dtype=jnp.int32)
    ranks = jnp.arange(B, dtype=jnp.int32)
    return jnp.where(ranks == 0, PIX - 1, jnp.where(ranks == 1, 0, drawn)).astype(jnp.int32)


def levels(rng, extent, cuts, smallest, largest):
    def one(dim, blocks):
        heights = jax.random.uniform(jax.random.fold_in(jax.random.fold_in(rng, 6), dim), (blocks,), jnp.float32, smallest / len(cuts), largest / len(cuts))
        return jnp.repeat(jnp.exp(heights), extent[dim] // blocks).reshape((-1,) + (1,) * (len(extent) - dim - 1))

    loudness = one(*cuts[0])
    for cut in cuts[1:]:
        loudness = loudness * one(*cut)
    return loudness


def centred(rng, extent, spread, bound, cuts=(), kind=jnp.bfloat16):
    array = jax.random.normal(rng, extent, jnp.float32) * spread
    if len(cuts) > 0:
        array = levels(rng, extent, cuts, -0.22, 0.18) * array
    return jnp.clip(array, min=-bound, max=bound).astype(kind)


def setup_inputs(seed: int = 0, part: int = 0) -> dict:
    key_list = jax.random.split(jax.random.key(seed), 5)
    part_splits = jax.random.split(jax.random.fold_in(key_list[4], part), 5)
    return {
        "voltages": draw_voltages(jax.random.fold_in(jax.random.fold_in(key_list[4], part), 71), part),
        "off_starts": draw_off_starts(jax.random.fold_in(jax.random.fold_in(key_list[4], part), 71), part),
        "pointing": draw_pointing(jax.random.fold_in(key_list[4], 71), part),
        "patterns": centred(key_list[3], (2, P_SIZE, PIX), (2 * P_SIZE) ** -0.5, 0.3125, ((2, 16),)),
    }


highest = lax.Precision.HIGHEST

def off_flags(starts):
    moments = jnp.arange(TIME, dtype=jnp.int32)
    inside = (moments[None, :] >= starts[:, None]) & (moments[None, :] < starts[:, None] + OFF_LEN)
    return jnp.any(inside, axis=0)

def beam_power(weights, patterns):
    real_rows = jnp.concatenate([weights[:, 0], weights[:, 1]], axis=-1)
    imag_rows = jnp.concatenate([-weights[:, 1], weights[:, 0]], axis=-1)
    rows_all = jnp.stack([real_rows, imag_rows], axis=2).reshape(-1, 2 * P_SIZE)
    response = jnp.dot(rows_all, patterns.reshape(2 * P_SIZE, -1), preferred_element_type=jnp.float32)
    response = response.reshape(weights.shape[0], weights.shape[2], 2, -1)
    return response[:, :, 0] * response[:, :, 0] + response[:, :, 1] * response[:, :, 1]

def reference(voltages, off_starts, pointing, patterns):
    is_off = off_flags(off_starts)
    off_count = jnp.sum(is_off.astype(jnp.float32))

    def channel_stats(channel_volts):
        samples = channel_volts.reshape(TIME, 2 * P_SIZE)
        on_source = jnp.where(is_off[:, None], jnp.zeros_like(samples), samples)
        products = lax.dot_general(on_source, samples, (((0,), (0,)), ((), ())), preferred_element_type=jnp.float32)
        corr_real = products[:P_SIZE, :P_SIZE] + products[P_SIZE:, P_SIZE:]
        corr_imag = products[P_SIZE:, :P_SIZE] - products[:P_SIZE, P_SIZE:]
        widened = samples.astype(jnp.float32)
        powers = lax.optimization_barrier(jnp.sum(jnp.where(is_off[:, None], widened * widened, jnp.float32(0.0)), axis=0))
        return (jnp.stack([corr_real, corr_imag]), powers[:P_SIZE] + powers[P_SIZE:])
    correlation, noise_sums = lax.map(channel_stats, voltages)
    noise_power = noise_sums / off_count + 1e-06
    scales = 1.0 / jnp.sqrt(noise_power)
    white_real = correlation[:, 0] * scales[:, :, None] * scales[:, None, :]
    white_imag = correlation[:, 1] * scales[:, :, None] * scales[:, None, :]
    steering = jnp.take(patterns, pointing, axis=2).astype(jnp.float32)
    steer_real = steering[0][None]
    steer_imag = steering[1][None]

    def apply_white(matrix, vector):
        return jnp.einsum('cij,cjb->cib', matrix, vector, precision=highest)

    def power_turn(counter, state_pair):
        beam_real, beam_imag = state_pair
        conj_real = steer_real * beam_real + steer_imag * beam_imag
        conj_imag = steer_real * beam_imag - steer_imag * beam_real
        mixed_real = apply_white(white_real, conj_real) - apply_white(white_imag, conj_imag)
        mixed_imag = apply_white(white_real, conj_imag) + apply_white(white_imag, conj_real)
        image_real = steer_real * mixed_real - steer_imag * mixed_imag
        image_imag = steer_real * mixed_imag + steer_imag * mixed_real
        mean_square = (lax.optimization_barrier(jnp.sum(image_real * image_real, axis=1)) + lax.optimization_barrier(jnp.sum(image_imag * image_imag, axis=1))) / (2 * P_SIZE)
        factor = 1.0 / jnp.sqrt(mean_square + 1e-06)
        return (image_real * factor[:, None, :], image_imag * factor[:, None, :])
    initial = (jnp.broadcast_to(steer_real, (CH, P_SIZE, B)), jnp.broadcast_to(steer_imag, (CH, P_SIZE, B)))
    beam_real, beam_imag = lax.fori_loop(0, ITERS, power_turn, initial)
    weight_real = beam_real * scales[:, :, None]
    weight_imag = beam_imag * scales[:, :, None]
    weights = jnp.stack([weight_real, weight_imag], axis=1).transpose(0, 1, 3, 2).astype(jnp.bfloat16)
    beam_weights = weights.reshape(CH, 2, B * P_SIZE)
    beam_maps = lax.map(lambda single: beam_power(single, patterns)[0], weights[:, None])
    return (beam_weights, beam_maps)
```

```python
import functools

import jax
import jax.numpy as jnp
from jax import lax
from jax.experimental import pallas as pl
from jax.experimental.pallas import tpu as pltpu
from jax.sharding import PartitionSpec as P

ITERS = 20
LANES = 128
SUB = 8
PAIR = 4


def lane_order(real, imag, axis):
    ports = real.shape[axis]
    full = ports // LANES * LANES
    tail = ports - full
    half = LANES // 2
    assert 0 < tail <= half
    blank = list(real.shape)
    blank[axis] = half - tail
    blank = jnp.zeros(blank, real.dtype)
    cut = functools.partial(lax.slice_in_dim, axis=axis)
    return jnp.concatenate(
        [cut(real, 0, full), cut(imag, 0, full), cut(real, full, ports), blank, cut(imag, full, ports), blank],
        axis=axis,
    )


def split_lanes(block, full):
    tails = block[:, 2 * full :]
    real = jnp.concatenate([block[:, :full], tails], axis=1)
    imag = jnp.concatenate([block[:, full : 2 * full], pltpu.roll(tails, LANES // 2, 1)], axis=1)
    return real, imag


def power_kernel(
    arr_ref, on_ref, count_ref, steer_ref, pay_ref, flat_ref, volt_ref, voltt_ref, scale_ref, lhs_ref, pay_sc, *, ports, group
):
    sources, channels, samples, wide = arr_ref.shape
    beams = steer_ref.shape[0]
    rows = volt_ref.shape[1] // 2
    full = ports // LANES * LANES
    width = full + LANES
    pad = lhs_ref.shape[1] // 4
    valid = lax.broadcasted_iota(jnp.int32, (beams, width), 1) < ports

    def padded(block):
        return jnp.concatenate([block, jnp.zeros((pad - beams, width), jnp.float32)], axis=0)

    steer_real, steer_imag = split_lanes(steer_ref[...].astype(jnp.float32), full)
    steer_real = padded(jnp.where(valid, steer_real, 0.0))
    steer_imag = padded(jnp.where(valid, steer_imag, 0.0))
    energy = steer_real * steer_real + steer_imag * steer_imag
    on = on_ref[...]

    def store_pair(k, both):
        high = both.astype(jnp.bfloat16)
        low = (both - high.astype(jnp.float32)).astype(jnp.bfloat16)
        lhs_ref[k, : 2 * pad] = high
        lhs_ref[k, 2 * pad :] = low

    def halves_dot(k_lhs, rhs):
        out = jnp.dot(k_lhs, rhs, preferred_element_type=jnp.float32)
        return out[: 2 * pad] + out[2 * pad :]

    def prepare(k, carry):
        block = arr_ref[:, pl.ds(k, 1)].astype(jnp.float32).reshape(rows, wide)
        kept = block * on
        gone = block - kept
        power = jnp.sum(gone * gone, axis=0, keepdims=True)
        power_real, power_imag = split_lanes(power, full)
        noise = (power_real + power_imag) / count_ref[0, 0] + 1e-06
        real, imag = split_lanes(kept, full)
        both = jnp.concatenate([real, imag], axis=0)
        volt_ref[k] = both.astype(jnp.bfloat16)
        voltt_ref[k] = both.T.astype(jnp.bfloat16)
        scale_ref[pl.ds(k, 1)] = (1.0 / noise)[None]
        first = energy * (1.0 / jnp.sqrt(noise))
        store_pair(k, jnp.concatenate([first, jnp.zeros_like(first)], axis=0))
        return carry

    lax.fori_loop(0, channels, prepare, 0)

    def apply_corr(k):
        part = halves_dot(lhs_ref[k], voltt_ref[k])
        real, imag = part[:pad], part[pad:]
        amp_real = real[:, :rows] + imag[:, rows:]
        amp_imag = imag[:, :rows] - real[:, rows:]
        both = jnp.concatenate(
            [jnp.concatenate([amp_real, -amp_imag], axis=1), jnp.concatenate([amp_imag, amp_real], axis=1)], axis=0
        )
        high = both.astype(jnp.bfloat16)
        low = (both - high.astype(jnp.float32)).astype(jnp.bfloat16)
        out = halves_dot(jnp.concatenate([high, low], axis=0), volt_ref[k])
        real, imag = out[:pad], out[pad:]
        weight = energy * scale_ref[k]
        scaled_real = weight * real
        scaled_imag = weight * imag
        mean = jnp.sum(scaled_real * real + scaled_imag * imag, axis=1, keepdims=True) / (2 * ports)
        factor = lax.rsqrt(mean + 1e-06)
        return real, imag, scaled_real, scaled_imag, factor

    def group_body(g, carry):
        def turn(step, inner):
            for j in range(group):
                k = g * group + j
                _, _, scaled_real, scaled_imag, factor = apply_corr(k)
                store_pair(k, jnp.concatenate([scaled_real * factor, scaled_imag * factor], axis=0))
            return inner

        lax.fori_loop(0, ITERS - 1, turn, 0)
        for j in range(group):
            k = g * group + j
            real, imag, _, _, factor = apply_corr(k)
            gain = scale_ref[k] * factor
            weight_real = ((steer_real * real - steer_imag * imag) * gain)[:beams]
            weight_imag = ((steer_real * imag + steer_imag * real) * gain)[:beams]
            flat_ref[k, 0] = weight_real[:, :ports].astype(jnp.bfloat16)
            flat_ref[k, 1] = weight_imag[:, :ports].astype(jnp.bfloat16)
            tails = weight_real[:, full:] + pltpu.roll(weight_imag[:, full:], LANES // 2, 1)
            tiles = [weight_real[:, i : i + LANES] for i in range(0, full, LANES)]
            tiles += [weight_imag[:, i : i + LANES] for i in range(0, full, LANES)]
            for i, tile in enumerate(tiles + [tails]):
                pay_sc[i, pl.ds(k, beams, stride=channels)] = tile
        return carry

    lax.fori_loop(0, channels // group, group_body, 0)
    for i in range(pay_sc.shape[0]):
        pay_ref[:, i * LANES : (i + 1) * LANES] = pay_sc[i].astype(jnp.bfloat16)


def power_weights(arrived, on, count, steer, ports):
    sources, channels, samples, wide = arrived.shape
    beams = steer.shape[0]
    rows = sources * samples
    width = ports // LANES * LANES + LANES
    pad = -(-beams // SUB) * SUB
    group = PAIR
    while channels % group:
        group //= 2
    return pl.pallas_call(
        functools.partial(power_kernel, ports=ports, group=group),
        out_shape=(
            jax.ShapeDtypeStruct((beams * channels, wide), jnp.bfloat16),
            jax.ShapeDtypeStruct((channels, 2, beams, ports), jnp.bfloat16),
        ),
        in_specs=[
            pl.BlockSpec(memory_space=pltpu.VMEM),
            pl.BlockSpec(memory_space=pltpu.VMEM),
            pl.BlockSpec(memory_space=pltpu.SMEM),
            pl.BlockSpec(memory_space=pltpu.VMEM),
        ],
        out_specs=(pl.BlockSpec(memory_space=pltpu.VMEM), pl.BlockSpec(memory_space=pltpu.VMEM)),
        scratch_shapes=[
            pltpu.VMEM((channels, 2 * rows, width), jnp.bfloat16),
            pltpu.VMEM((channels, width, 2 * rows), jnp.bfloat16),
            pltpu.VMEM((channels, 1, width), jnp.float32),
            pltpu.VMEM((channels, 4 * pad, width), jnp.bfloat16),
            pltpu.VMEM((wide // LANES, beams * channels, LANES), jnp.float32),
        ],
        name="power",
    )(arrived, on, count, steer)


def maps_kernel(w_ref, p_ref, o_ref):
    devices, block, channels, wide = w_ref.shape
    pixels = o_ref.shape[2]
    taps = p_ref[...]
    for b in range(block):
        rows = w_ref[:, b].reshape(devices * channels, wide)
        response = jnp.dot(rows, taps, preferred_element_type=jnp.float32)
        real, imag = response[:, :pixels], response[:, pixels:]
        o_ref[b] = real * real + imag * imag


def beam_power(gathered, taps):
    devices, beams, channels, wide = gathered.shape
    pixels = taps.shape[1] // 2
    block = 4
    while beams % block:
        block //= 2
    return pl.pallas_call(
        maps_kernel,
        grid=(beams // block,),
        out_shape=jax.ShapeDtypeStruct((beams, devices * channels, pixels), jnp.float32),
        in_specs=[
            pl.BlockSpec((devices, block, channels, wide), lambda i: (0, i, 0, 0)),
            pl.BlockSpec(taps.shape, lambda i: (0, 0)),
        ],
        out_specs=pl.BlockSpec((block, devices * channels, pixels), lambda i: (i, 0, 0)),
        name="maps",
    )(gathered, taps)


def off_flags(moments, starts, range_len):
    inside = (moments[None, :] >= starts[:, None]) & (moments[None, :] < starts[:, None] + range_len)
    return jnp.any(inside, axis=0)


def sum_over(value, axis, devices):
    if devices & (devices - 1):
        return lax.psum(value, axis)
    step = 1
    while step < devices:
        value = value + lax.ppermute(value, axis, [(i, i ^ step) for i in range(devices)])
        step *= 2
    return value


def on_device(voltages, off_starts, pointing, patterns):
    devices = lax.axis_size("tm")
    position = lax.axis_index("tm")
    channels, samples_dev, _, ports = voltages.shape
    beams = pointing.shape[0]
    per_dev = channels // devices
    total_time = samples_dev * devices
    off_span = max(4, total_time // 32)
    is_off = off_flags(jnp.arange(total_time, dtype=jnp.int32), off_starts, off_span)
    off_count = jnp.sum(is_off.astype(jnp.float32)).reshape(1, 1)
    on = 1.0 - is_off.astype(jnp.float32)[:, None]

    pixels = patterns.shape[2]
    real, imag = patterns[0], patterns[1]
    ordered = lane_order(real, imag, 0)
    taps = jnp.concatenate([ordered, lane_order(imag, -real, 0)], axis=1)
    pixel_ids = position * pixels + jnp.arange(pixels, dtype=jnp.int32)
    selector = (pointing[:, None] == pixel_ids[None, :]).astype(jnp.bfloat16)
    steer_local = jnp.einsum("bx,lx->bl", selector, ordered, preferred_element_type=jnp.float32)
    steering = sum_over(steer_local.astype(jnp.bfloat16), "tm", devices)

    packed = lane_order(voltages[:, :, 0], voltages[:, :, 1], 2)
    blocks = packed.reshape(devices, per_dev, samples_dev, packed.shape[-1])
    arrived = lax.all_to_all(blocks, "tm", split_axis=0, concat_axis=0, tiled=True)
    payload, weights = power_weights(arrived, on, off_count, steering, ports)
    flat_pair = weights.reshape(per_dev, 2, beams * ports)
    collected = lax.all_gather(payload, "tm", axis=0, tiled=False)
    maps = beam_power(collected.reshape(devices, beams, per_dev, -1), taps)
    return (flat_pair, maps.transpose(1, 0, 2))


def solution(mesh):
    in_specs = (P(None, ("groups", "tm"), None, None), P("groups"), P(), P(None, None, "tm"))
    out_specs = (P(("groups", "tm"), None, None), P("groups", None, "tm"))
    return jax.shard_map(on_device, mesh=mesh, in_specs=in_specs, out_specs=out_specs, check_vma=False)
```

```python
import functools

import jax
import jax.numpy as jnp
from jax import lax
from jax.experimental import pallas as pl
from jax.experimental.pallas import tpu as pltpu
from jax.sharding import PartitionSpec as P


ITERS = 20
LANES = 128
SUB = 8
PAIR = 16
TURNS = 3
CHUNKS = 2


def lane_order(real, imag, axis):
    ports = real.shape[axis]
    full = ports // LANES * LANES
    tail = ports - full
    half = LANES // 2
    assert 0 < tail <= half
    blank = list(real.shape)
    blank[axis] = half - tail
    blank = jnp.zeros(blank, real.dtype)
    cut = functools.partial(lax.slice_in_dim, axis=axis)
    return jnp.concatenate(
        [cut(real, 0, full), cut(imag, 0, full), cut(real, full, ports), blank, cut(imag, full, ports), blank],
        axis=axis,
    )


def split_lanes(block, full):
    tails = block[:, 2 * full :]
    real = jnp.concatenate([block[:, :full], tails], axis=1)
    imag = jnp.concatenate([block[:, full : 2 * full], pltpu.roll(tails, LANES // 2, 1)], axis=1)
    return real, imag


def power_kernel(
    arr_ref, on_ref, count_ref, steer_ref, pay_ref, flat_ref, volt_ref, voltt_ref, scale_ref, lhs_ref, pay_sc, *, ports, group
):
    _, channels, _, wide = arr_ref.shape
    beams = steer_ref.shape[0]
    rows = volt_ref.shape[1] // 2
    full = ports // LANES * LANES
    width = full + LANES
    pad = lhs_ref.shape[1] // 4
    valid = lax.broadcasted_iota(jnp.int32, (beams, width), 1) < ports

    def padded(block):
        if pad == beams:
            return block
        return jnp.concatenate([block, jnp.zeros((pad - beams, width), jnp.float32)], axis=0)

    steer_real, steer_imag = split_lanes(steer_ref[...].astype(jnp.float32), full)
    steer_real = padded(jnp.where(valid, steer_real, 0.0))
    steer_imag = padded(jnp.where(valid, steer_imag, 0.0))
    energy = steer_real * steer_real + steer_imag * steer_imag
    on = on_ref[...]

    def store_pair(k, both):
        high = both.astype(jnp.bfloat16)
        low = (both - high.astype(jnp.float32)).astype(jnp.bfloat16)
        lhs_ref[k, : 2 * pad] = high
        lhs_ref[k, 2 * pad :] = low

    def halves_dot(k_lhs, rhs):
        out = jnp.dot(k_lhs, rhs, preferred_element_type=jnp.float32)
        return out[: 2 * pad] + out[2 * pad :]

    def prepare(k, carry):
        block = arr_ref[:, pl.ds(k, 1)].astype(jnp.float32).reshape(rows, wide)
        kept = block * on
        gone = block - kept
        power = jnp.sum(gone * gone, axis=0, keepdims=True)
        power_real, power_imag = split_lanes(power, full)
        noise = (power_real + power_imag) / count_ref[0, 0] + 1e-06
        real, imag = split_lanes(kept, full)
        both = jnp.concatenate([real, imag], axis=0)
        volt_ref[k] = both.astype(jnp.bfloat16)
        voltt_ref[k] = both.T.astype(jnp.bfloat16)
        scale_ref[pl.ds(k, 1)] = (1.0 / noise)[None]
        first = energy * (1.0 / jnp.sqrt(noise))
        store_pair(k, jnp.concatenate([first, jnp.zeros_like(first)], axis=0))
        return carry

    lax.fori_loop(0, channels, prepare, 0, unroll=min(4, channels))

    def apply_corr(k):
        part = halves_dot(lhs_ref[k], voltt_ref[k])
        real, imag = part[:pad], part[pad:]
        amp_real = real[:, :rows] + imag[:, rows:]
        amp_imag = imag[:, :rows] - real[:, rows:]
        both = jnp.concatenate(
            [jnp.concatenate([amp_real, -amp_imag], axis=1), jnp.concatenate([amp_imag, amp_real], axis=1)], axis=0
        )
        high = both.astype(jnp.bfloat16)
        low = (both - high.astype(jnp.float32)).astype(jnp.bfloat16)
        out = halves_dot(jnp.concatenate([high, low], axis=0), volt_ref[k])
        real, imag = out[:pad], out[pad:]
        weight = energy * scale_ref[k]
        scaled_real = weight * real
        scaled_imag = weight * imag
        mean = jnp.sum(scaled_real * real + scaled_imag * imag, axis=1, keepdims=True) / (2 * ports)
        factor = lax.rsqrt(mean + 1e-06)
        return real, imag, scaled_real, scaled_imag, factor

    def group_body(g, carry):
        def turn():
            for j in range(group):
                k = g * group + j
                _, _, scaled_real, scaled_imag, factor = apply_corr(k)
                store_pair(k, jnp.concatenate([scaled_real * factor, scaled_imag * factor], axis=0))

        def trip(step, inner):
            for _ in range(TURNS):
                turn()
            return inner

        lax.fori_loop(0, (ITERS - 1) // TURNS, trip, 0)
        for _ in range((ITERS - 1) % TURNS):
            turn()
        for j in range(group):
            k = g * group + j
            real, imag, _, _, factor = apply_corr(k)
            gain = scale_ref[k] * factor
            weight_real = ((steer_real * real - steer_imag * imag) * gain)[:beams]
            weight_imag = ((steer_real * imag + steer_imag * real) * gain)[:beams]
            flat_ref[k, 0] = weight_real[:, :ports].astype(jnp.bfloat16)
            flat_ref[k, 1] = weight_imag[:, :ports].astype(jnp.bfloat16)
            tails = weight_real[:, full:] + pltpu.roll(weight_imag[:, full:], LANES // 2, 1)
            tiles = [weight_real[:, i : i + LANES] for i in range(0, full, LANES)]
            tiles += [weight_imag[:, i : i + LANES] for i in range(0, full, LANES)]
            for i, tile in enumerate(tiles + [tails]):
                pay_sc[i, pl.ds(k, beams, stride=channels)] = tile
        return carry

    lax.fori_loop(0, channels // group, group_body, 0)
    for i in range(pay_sc.shape[0]):
        pay_ref[:, i * LANES : (i + 1) * LANES] = pay_sc[i].astype(jnp.bfloat16)


def power_weights(arrived, on, count, steer, ports):
    sources, channels, samples, wide = arrived.shape
    beams = steer.shape[0]
    rows = sources * samples
    width = ports // LANES * LANES + LANES
    pad = -(-beams // SUB) * SUB
    group = PAIR
    while channels % group:
        group //= 2
    return pl.pallas_call(
        functools.partial(power_kernel, ports=ports, group=group),
        out_shape=(
            jax.ShapeDtypeStruct((beams * channels, wide), jnp.bfloat16),
            jax.ShapeDtypeStruct((channels, 2, beams, ports), jnp.bfloat16),
        ),
        in_specs=[
            pl.BlockSpec(memory_space=pltpu.VMEM),
            pl.BlockSpec(memory_space=pltpu.VMEM),
            pl.BlockSpec(memory_space=pltpu.SMEM),
            pl.BlockSpec(memory_space=pltpu.VMEM),
        ],
        out_specs=(pl.BlockSpec(memory_space=pltpu.VMEM), pl.BlockSpec(memory_space=pltpu.VMEM)),
        scratch_shapes=[
            pltpu.VMEM((channels, 2 * rows, width), jnp.bfloat16),
            pltpu.VMEM((channels, width, 2 * rows), jnp.bfloat16),
            pltpu.VMEM((channels, 1, width), jnp.float32),
            pltpu.VMEM((channels, 4 * pad, width), jnp.bfloat16),
            pltpu.VMEM((wide // LANES, beams * channels, LANES), jnp.float32),
        ],
        name="power",
    )(arrived, on, count, steer)


def maps_kernel(ids_ref, taps_ref, *refs, shards, views, channels, first, per_dev, begun):
    shard_refs = refs[:shards]
    out_ref, *sent_refs = refs[shards + begun : shards + begun + views]
    in_buf, out_buf, in_sem, out_sem = refs[-4:]
    pixels = out_buf.shape[3]
    each = shard_refs[0].shape[0]

    def fetch(op, i, slot):
        return pltpu.make_async_copy(shard_refs[op].at[i], in_buf.at[slot], in_sem.at[slot])

    def emit(step, slot):
        row = pl.multiple_of(ids_ref[step] * per_dev + first, channels)
        return pltpu.make_async_copy(out_buf.at[slot], out_ref.at[:, pl.ds(row, channels)], out_sem.at[slot])

    def view(rows, j):
        taps = taps_ref[:, 2 * j * pixels : 2 * (j + 1) * pixels]
        response = jnp.dot(rows, taps, preferred_element_type=jnp.float32)
        real, imag = response[:, :pixels], response[:, pixels:]
        return real * real + imag * imag

    if each == 1:
        for step in range(shards):
            fetch(step, 0, step).start()
        for step in range(shards):
            fetch(step, 0, step).wait()
            rows = in_buf[step]
            out_buf[step] = view(rows, 0).reshape(out_buf.shape[1:])
            emit(step, step).start()
            for j, sent in enumerate(sent_refs):
                sent[step] = view(rows, j + 1).astype(jnp.bfloat16)
        for step in range(shards):
            emit(step, step).wait()
    else:

        def body(step, carry):
            copy = fetch(0, step, 0)
            copy.start()
            copy.wait()
            out_buf[0] = view(in_buf[0], 0).reshape(out_buf.shape[1:])
            out = emit(step, 0)
            out.start()
            out.wait()
            return carry

        lax.fori_loop(0, each, body, 0)


def beam_power(ids, taps, shards, into, shape, channels, first, per_dev):
    beams, _, pixels = shape
    each, depth, wide = shards[0].shape
    assert each == 1 or len(shards) == 1
    views = taps.shape[1] // (2 * pixels)
    begun = into is not None
    any_space = pl.BlockSpec(memory_space=pl.ANY)
    vmem = pl.BlockSpec(memory_space=pltpu.VMEM)
    operands = [ids, taps, *shards] + ([into] if begun else [])
    sent = jax.ShapeDtypeStruct((len(shards), depth, pixels), jnp.bfloat16)
    slots = len(shards)
    return pl.pallas_call(
        functools.partial(
            maps_kernel, shards=slots, views=views, channels=channels, first=first, per_dev=per_dev, begun=begun
        ),
        out_shape=(jax.ShapeDtypeStruct(shape, jnp.float32),) + (sent,) * (views - 1),
        in_specs=[pl.BlockSpec(memory_space=pltpu.SMEM), vmem] + [any_space] * (len(operands) - 2),
        out_specs=(any_space,) + (vmem,) * (views - 1),
        scratch_shapes=[
            pltpu.VMEM((slots, depth, wide), jnp.bfloat16),
            pltpu.VMEM((slots, beams, channels, pixels), jnp.float32),
            pltpu.SemaphoreType.DMA((slots,)),
            pltpu.SemaphoreType.DMA((slots,)),
        ],
        input_output_aliases={2 + slots: 0} if begun else {},
        name="maps",
    )(*operands)


def place_kernel(ids_ref, *refs, parts, channels, first, per_dev):
    part_refs = refs[:parts]
    out_ref, buf, sem = refs[parts + 1], refs[-2], refs[-1]
    each = part_refs[0].shape[0]

    def emit(slot):
        row = pl.multiple_of(ids_ref[slot] * per_dev + first, channels)
        return pltpu.make_async_copy(buf.at[slot], out_ref.at[:, pl.ds(row, channels)], sem.at[slot])

    for op, part in enumerate(part_refs):
        for i in range(each):
            slot = op * each + i
            buf[slot] = part[i].astype(jnp.float32).reshape(buf.shape[1:])
            emit(slot).start()
    for slot in range(parts * each):
        emit(slot).wait()


def place_maps(ids, parts, into, channels, first, per_dev):
    beams, _, pixels = into.shape
    slots = len(parts) * parts[0].shape[0]
    any_space = pl.BlockSpec(memory_space=pl.ANY)
    return pl.pallas_call(
        functools.partial(place_kernel, parts=len(parts), channels=channels, first=first, per_dev=per_dev),
        out_shape=jax.ShapeDtypeStruct(into.shape, jnp.float32),
        in_specs=[pl.BlockSpec(memory_space=pltpu.SMEM)]
        + [pl.BlockSpec(memory_space=pltpu.VMEM)] * len(parts)
        + [any_space],
        out_specs=any_space,
        scratch_shapes=[
            pltpu.VMEM((slots, beams, channels, pixels), jnp.float32),
            pltpu.SemaphoreType.DMA((slots,)),
        ],
        input_output_aliases={1 + len(parts): 0},
        name="place",
    )(ids, *parts, into)


def off_flags(moments, starts, range_len):
    inside = (moments[None, :] >= starts[:, None]) & (moments[None, :] < starts[:, None] + range_len)
    return jnp.any(inside, axis=0)


def sum_over(value, axis, devices):
    if devices & (devices - 1):
        return lax.psum(value, axis)
    step = 1
    while step < devices:
        moved = lax.ppermute(value, axis, [(i, i ^ step) for i in range(devices)])
        value = value + moved
        step *= 2
    return value


def turned(value, shift, count):
    return lax.ppermute(value, "tm", [(i, (i + shift) % count) for i in range(count)])


def crossed(value, bits, count):
    return lax.ppermute(value, "tm", [(i, i ^ bits) for i in range(count)])


def other_parts(ordered, full):
    half = LANES // 2
    real, imag, tails = ordered[:full], ordered[full : 2 * full], ordered[2 * full :]
    return jnp.concatenate([imag, -real, tails[half:], -tails[:half]], axis=0)


def on_device(voltages, off_starts, pointing, patterns):
    devices = lax.axis_size("tm")
    position = lax.axis_index("tm")
    channels, samples_dev, _, ports = voltages.shape
    beams = pointing.shape[0]
    per_dev = channels // devices
    full = ports // LANES * LANES
    total_time = samples_dev * devices
    off_span = max(4, total_time // 32)
    is_off = off_flags(jnp.arange(total_time, dtype=jnp.int32), off_starts, off_span)
    off_count = jnp.sum(is_off.astype(jnp.float32)).reshape(1, 1)
    on = 1.0 - is_off.astype(jnp.float32)[:, None]

    pixels = patterns.shape[2]
    ordered = lane_order(patterns[0], patterns[1], 0)
    pixel_ids = position * pixels + jnp.arange(pixels, dtype=jnp.int32)
    selector = (pointing[:, None] == pixel_ids[None, :]).astype(jnp.bfloat16)
    steer_local = jnp.einsum("bx,lx->bl", selector, ordered, preferred_element_type=jnp.float32)
    steering = sum_over(steer_local.astype(jnp.bfloat16), "tm", devices)

    packed = lane_order(voltages[:, :, 0], voltages[:, :, 1], 2)
    blocks = packed.reshape(devices, per_dev, samples_dev, packed.shape[-1])
    lines = devices == 16 and per_dev % (8 * CHUNKS) == 0
    chunks = CHUNKS if lines else 1
    part = per_dev // chunks
    shape = (beams, channels, pixels)

    arrived = []
    for i in range(chunks):
        block = blocks[:, i * part : (i + 1) * part]
        arrived.append(lax.all_to_all(block, "tm", split_axis=0, concat_axis=0, tiled=True))
    taps = [ordered]
    if lines:
        taps += [crossed(ordered, bits, devices) for bits in (1, 2, 3)]
    taps = jnp.concatenate([t for o in taps for t in (o, other_parts(o, full))], axis=1)

    outs = []
    for block in arrived:
        outs.append(power_weights(block, on, off_count, steering, ports))
    weights = jnp.concatenate([w for _, w in outs], axis=0)
    flat_pair = weights.reshape(per_dev, 2, beams * ports)
    if lines:
        shifts = (0, 4, 12, 8)
        sources = jnp.stack([(position - shift) % devices for shift in shifts]).astype(jnp.int32)
        maps = None
        sent = []
        for i, (payload, _) in enumerate(outs):
            shards = [payload] + [turned(payload, shift, devices) for shift in shifts[1:]]
            maps, *away = beam_power(
                sources, taps, [shard[None] for shard in shards], maps, shape, part, i * part, per_dev
            )
            sent.append([crossed(away[bits - 1], bits, devices) for bits in (2, 3, 1)])
        places = jnp.concatenate([sources ^ bits for bits in (2, 3, 1)])
        for i, parts in enumerate(sent):
            maps = place_maps(places, parts, maps, part, i * part, per_dev)
    else:
        collected = lax.all_gather(outs[0][0], "tm", axis=0, tiled=False)
        (maps,) = beam_power(jnp.arange(devices, dtype=jnp.int32), taps, [collected], None, shape, part, 0, per_dev)
    return (flat_pair, maps.transpose(1, 0, 2))


def solution(mesh):
    in_specs = (P(None, ("groups", "tm"), None, None), P("groups"), P(), P(None, None, "tm"))
    out_specs = (P(("groups", "tm"), None, None), P("groups", None, "tm"))
    return jax.shard_map(on_device, mesh=mesh, in_specs=in_specs, out_specs=out_specs, check_vma=False)
```

```python
import functools

import jax
import jax.numpy as jnp
from jax import lax
from jax.experimental import pallas as pl
from jax.experimental.pallas import tpu as pltpu
from jax.sharding import PartitionSpec as P


ITERS = 20
LANES = 128
SUB = 8
PAIR = 16
TURNS = 3
GRANT = pltpu.CompilerParams(vmem_limit_bytes=28 << 20)
MAP_SLOTS = 16
CHUNKS = 2


def lane_order(real, imag, axis):
    ports = real.shape[axis]
    full = ports // LANES * LANES
    tail = ports - full
    half = LANES // 2
    assert 0 < tail <= half
    blank = list(real.shape)
    blank[axis] = half - tail
    blank = jnp.zeros(blank, real.dtype)
    cut = functools.partial(lax.slice_in_dim, axis=axis)
    return jnp.concatenate(
        [cut(real, 0, full), cut(imag, 0, full), cut(real, full, ports), blank, cut(imag, full, ports), blank],
        axis=axis,
    )


def lane_places(ports):
    full = ports // LANES * LANES
    part = jnp.arange(2)[:, None]
    port = jnp.arange(ports)[None, :]
    place = jnp.where(port < full, part * full + port, full + port + part * (LANES // 2))
    return (place[:, :, None] == jnp.arange(2 * full + LANES)).astype(jnp.bfloat16)


def split_lanes(block, full):
    tails = block[:, 2 * full :]
    real = jnp.concatenate([block[:, :full], tails], axis=1)
    imag = jnp.concatenate([block[:, full : 2 * full], pltpu.roll(tails, LANES // 2, 1)], axis=1)
    return real, imag


def power_kernel(
    arr_ref, on_ref, count_ref, steer_ref, pay_ref, flat_ref, volt_ref, voltt_ref, scale_ref, lhs_ref, pay_sc, *, ports, group
):
    _, channels, _, wide = arr_ref.shape
    beams = steer_ref.shape[0]
    rows = volt_ref.shape[1] // 2
    full = ports // LANES * LANES
    width = full + LANES
    pad = lhs_ref.shape[1] // 4
    valid = lax.broadcasted_iota(jnp.int32, (beams, width), 1) < ports

    def padded(block):
        if pad == beams:
            return block
        return jnp.concatenate([block, jnp.zeros((pad - beams, width), jnp.float32)], axis=0)

    steer_real, steer_imag = split_lanes(steer_ref[...].astype(jnp.float32), full)
    steer_real = padded(jnp.where(valid, steer_real, 0.0))
    steer_imag = padded(jnp.where(valid, steer_imag, 0.0))
    energy = steer_real * steer_real + steer_imag * steer_imag
    on = on_ref[...]

    def store_pair(k, both):
        high = both.astype(jnp.bfloat16)
        low = (both - high.astype(jnp.float32)).astype(jnp.bfloat16)
        lhs_ref[k, : 2 * pad] = high
        lhs_ref[k, 2 * pad :] = low

    def halves_dot(k_lhs, rhs):
        out = jnp.dot(k_lhs, rhs, preferred_element_type=jnp.float32)
        return out[: 2 * pad] + out[2 * pad :]

    def prepare(k, carry):
        block = arr_ref[:, pl.ds(k, 1)].astype(jnp.float32).reshape(rows, wide)
        kept = block * on
        gone = block - kept
        power = jnp.sum(gone * gone, axis=0, keepdims=True)
        power_real, power_imag = split_lanes(power, full)
        noise = (power_real + power_imag) / count_ref[0, 0] + 1e-06
        real, imag = split_lanes(kept, full)
        both = jnp.concatenate([real, imag], axis=0)
        volt_ref[k] = both.astype(jnp.bfloat16)
        voltt_ref[k] = both.T.astype(jnp.bfloat16)
        scale_ref[pl.ds(k, 1)] = (1.0 / noise)[None]
        first = energy * (1.0 / jnp.sqrt(noise))
        store_pair(k, jnp.concatenate([first, jnp.zeros_like(first)], axis=0))
        return carry

    lax.fori_loop(0, channels, prepare, 0, unroll=min(4, channels))

    def apply_corr(k):
        part = halves_dot(lhs_ref[k], voltt_ref[k])
        real, imag = part[:pad], part[pad:]
        amp_real = real[:, :rows] + imag[:, rows:]
        amp_imag = imag[:, :rows] - real[:, rows:]
        both = jnp.concatenate(
            [jnp.concatenate([amp_real, -amp_imag], axis=1), jnp.concatenate([amp_imag, amp_real], axis=1)], axis=0
        )
        high = both.astype(jnp.bfloat16)
        low = (both - high.astype(jnp.float32)).astype(jnp.bfloat16)
        out = halves_dot(jnp.concatenate([high, low], axis=0), volt_ref[k])
        real, imag = out[:pad], out[pad:]
        weight = energy * scale_ref[k]
        scaled_real = weight * real
        scaled_imag = weight * imag
        mean = jnp.sum(scaled_real * real + scaled_imag * imag, axis=1, keepdims=True) / (2 * ports)
        factor = lax.rsqrt(mean + 1e-06)
        return real, imag, scaled_real, scaled_imag, factor

    def group_body(g, carry):
        def turn():
            for j in range(group):
                k = g * group + j
                _, _, scaled_real, scaled_imag, factor = apply_corr(k)
                store_pair(k, jnp.concatenate([scaled_real * factor, scaled_imag * factor], axis=0))

        def trip(step, inner):
            for _ in range(TURNS):
                turn()
            return inner

        lax.fori_loop(0, (ITERS - 1) // TURNS, trip, 0)
        for _ in range((ITERS - 1) % TURNS):
            turn()
        for j in range(group):
            k = g * group + j
            real, imag, _, _, factor = apply_corr(k)
            gain = scale_ref[k] * factor
            weight_real = ((steer_real * real - steer_imag * imag) * gain)[:beams]
            weight_imag = ((steer_real * imag + steer_imag * real) * gain)[:beams]
            flat_ref[k, 0] = weight_real[:, :ports].astype(jnp.bfloat16)
            flat_ref[k, 1] = weight_imag[:, :ports].astype(jnp.bfloat16)
            tails = weight_real[:, full:] + pltpu.roll(weight_imag[:, full:], LANES // 2, 1)
            tiles = [weight_real[:, i : i + LANES] for i in range(0, full, LANES)]
            tiles += [weight_imag[:, i : i + LANES] for i in range(0, full, LANES)]
            for i, tile in enumerate(tiles + [tails]):
                pay_sc[i, pl.ds(k, beams, stride=channels)] = tile
        return carry

    lax.fori_loop(0, channels // group, group_body, 0)
    for i in range(pay_sc.shape[0]):
        pay_ref[:, i * LANES : (i + 1) * LANES] = pay_sc[i].astype(jnp.bfloat16)


def here(value):
    return pltpu.with_memory_space_constraint(value, pltpu.VMEM)


def power_weights(arrived, on, count, steer, ports):
    sources, channels, samples, wide = arrived.shape
    beams = steer.shape[0]
    rows = sources * samples
    width = ports // LANES * LANES + LANES
    pad = -(-beams // SUB) * SUB
    group = PAIR
    while channels % group:
        group //= 2
    return pl.pallas_call(
        functools.partial(power_kernel, ports=ports, group=group),
        out_shape=(
            jax.ShapeDtypeStruct((beams * channels, wide), jnp.bfloat16),
            jax.ShapeDtypeStruct((channels, 2, beams, ports), jnp.bfloat16),
        ),
        in_specs=[
            pl.BlockSpec(memory_space=pltpu.VMEM),
            pl.BlockSpec(memory_space=pltpu.VMEM),
            pl.BlockSpec(memory_space=pltpu.SMEM),
            pl.BlockSpec(memory_space=pltpu.VMEM),
        ],
        out_specs=(pl.BlockSpec(memory_space=pltpu.VMEM), pl.BlockSpec(memory_space=pltpu.VMEM)),
        scratch_shapes=[
            pltpu.VMEM((channels, 2 * rows, width), jnp.bfloat16),
            pltpu.VMEM((channels, width, 2 * rows), jnp.bfloat16),
            pltpu.VMEM((channels, 1, width), jnp.float32),
            pltpu.VMEM((channels, 4 * pad, width), jnp.bfloat16),
            pltpu.VMEM((wide // LANES, beams * channels, LANES), jnp.float32),
        ],
        compiler_params=GRANT,
        name="power",
    )(here(arrived), on, count, steer)


def other_parts(ordered):
    half = LANES // 2
    full = (ordered.shape[0] - LANES) // 2
    real, imag, tails = ordered[:full], ordered[full : 2 * full], ordered[2 * full :]
    return jnp.concatenate([imag, -real, tails[half:], -tails[:half]], axis=0)


def view(rows, ordered):
    pixels = ordered.shape[1]
    taps = jnp.concatenate([ordered, other_parts(ordered)], axis=1)
    response = jnp.dot(rows, taps, preferred_element_type=jnp.float32)
    real, imag = response[:, :pixels], response[:, pixels:]
    return real * real + imag * imag


def away_kernel(*refs, shards, views):
    shard_refs, taps_refs, sent_refs = refs[:shards], refs[shards : shards + views], refs[shards + views :]
    for taps, sent in zip(taps_refs, sent_refs):
        for step, shard in enumerate(shard_refs):
            sent[step] = view(shard[...], taps[...]).astype(jnp.bfloat16)


def away_maps(taps, shards):
    depth, _ = shards[0].shape
    pixels = taps[0].shape[1]
    views = len(taps)
    sent = jax.ShapeDtypeStruct((len(shards), depth, pixels), jnp.bfloat16)
    vmem = pl.BlockSpec(memory_space=pltpu.VMEM)
    return pl.pallas_call(
        functools.partial(away_kernel, shards=len(shards), views=views),
        out_shape=(sent,) * views,
        in_specs=[vmem] * (views + len(shards)),
        out_specs=(vmem,) * views,
        compiler_params=GRANT,
        name="away",
    )(*[here(shard) for shard in shards], *taps)


def write_kernel(rows_ref, *refs, parts, channels, with_taps, begun):
    taps_ref = refs[0] if with_taps else None
    part_refs = refs[with_taps : with_taps + parts]
    out_ref = refs[with_taps + parts + begun]
    buf, sem = refs[-2:]
    each = part_refs[0].shape[0]
    slots = buf.shape[0]

    def emit(step, slot):
        row = pl.multiple_of(rows_ref[step], channels)
        return pltpu.make_async_copy(buf.at[slot], out_ref.at[:, pl.ds(row, channels)], sem.at[slot])

    def work(piece, slot):
        piece = view(piece, taps_ref[...]) if with_taps else piece.astype(jnp.float32)
        buf[slot] = piece.reshape(buf.shape[1:])

    if slots == parts * each:
        for step in range(slots):
            work(part_refs[step // each][step % each], step)
            emit(step, step).start()
        for step in range(slots):
            emit(step, step).wait()
    else:

        def body(step, carry):
            work(part_refs[0][step], 0)
            out = emit(step, 0)
            out.start()
            out.wait()
            return carry

        lax.fori_loop(0, each, body, 0)


def write_maps(rows, parts, into, shape, channels, taps=None):
    beams, _, pixels = shape
    slots = parts[0].shape[0] * len(parts)
    if slots > MAP_SLOTS:
        assert len(parts) == 1
        slots = 1
    any_space = pl.BlockSpec(memory_space=pl.ANY)
    near = ([] if taps is None else [taps]) + [here(part) if slots > 1 else part for part in parts]
    tails = [] if into is None else [into]
    return pl.pallas_call(
        functools.partial(
            write_kernel,
            parts=len(parts),
            channels=channels,
            with_taps=len(near) - len(parts),
            begun=len(tails),
        ),
        out_shape=jax.ShapeDtypeStruct(shape, jnp.float32),
        in_specs=[pl.BlockSpec(memory_space=pltpu.SMEM)]
        + [pl.BlockSpec(memory_space=pltpu.VMEM)] * len(near)
        + [any_space] * len(tails),
        out_specs=any_space,
        scratch_shapes=[
            pltpu.VMEM((slots, beams, channels, pixels), jnp.float32),
            pltpu.SemaphoreType.DMA((slots,)),
        ],
        input_output_aliases={1 + len(near): 0} if tails else {},
        compiler_params=GRANT,
        name="write",
    )(rows, *near, *tails)


def off_flags(moments, starts, range_len):
    inside = (moments[None, :] >= starts[:, None]) & (moments[None, :] < starts[:, None] + range_len)
    return jnp.any(inside, axis=0)


def sum_over(value, devices, lines):
    if devices & (devices - 1):
        return lax.psum(value, "tm")
    step = 1
    while step < (4 if lines else devices):
        moved = crossed(value, step, devices)
        value = value + moved
        step *= 2
    if lines:
        moved = [turned(value, shift, devices) for shift in (4, 12, 8)]
        value = (value + moved[0]) + (moved[1] + moved[2])
    return value


def turned(value, shift, count):
    return lax.ppermute(value, "tm", [(i, (i + shift) % count) for i in range(count)])


def crossed(value, bits, count):
    return lax.ppermute(value, "tm", [(i, i ^ bits) for i in range(count)])


def on_device(voltages, off_starts, pointing, patterns):
    devices = lax.axis_size("tm")
    position = lax.axis_index("tm")
    channels, samples_dev, _, ports = voltages.shape
    beams = pointing.shape[0]
    per_dev = channels // devices
    full = ports // LANES * LANES
    total_time = samples_dev * devices
    off_span = max(4, total_time // 32)
    is_off = off_flags(jnp.arange(total_time, dtype=jnp.int32), off_starts, off_span)
    off_count = jnp.sum(is_off.astype(jnp.float32)).reshape(1, 1)
    on = 1.0 - is_off.astype(jnp.float32)[:, None]

    pixels = patterns.shape[2]
    ordered = lane_order(patterns[0], patterns[1], 0)
    pixel_ids = position * pixels + jnp.arange(pixels, dtype=jnp.int32)
    selector = (pointing[:, None] == pixel_ids[None, :]).astype(jnp.bfloat16)
    steer_local = jnp.einsum("bx,lx->bl", selector, ordered, preferred_element_type=jnp.float32)
    lines = devices == 16 and per_dev % (8 * CHUNKS) == 0
    steering = sum_over(steer_local.astype(jnp.bfloat16), devices, lines)

    wide = 2 * full + LANES
    packed = jnp.einsum("ctrp,rpl->ctl", voltages, lane_places(ports), preferred_element_type=jnp.float32)
    blocks = packed.astype(jnp.bfloat16).reshape(devices, per_dev, samples_dev, wide)
    chunks = CHUNKS if lines else 1
    part = per_dev // chunks
    shape = (beams, channels, pixels)

    arrived = []
    for i in range(chunks):
        block = blocks[:, i * part : (i + 1) * part]
        arrived.append(lax.all_to_all(block, "tm", split_axis=0, concat_axis=0, tiled=True))
    near = (2, 3, 1)
    if lines:
        others = [crossed(ordered, bits, devices) for bits in near]

    outs = []
    for block in arrived:
        outs.append(power_weights(block, on, off_count, steering, ports))
    weights = jnp.concatenate([w for _, w in outs], axis=0)
    flat_pair = weights.reshape(per_dev, 2, beams * ports)
    if lines:
        shifts = (0, 4, 12, 8)
        sources = jnp.stack([(position - shift) % devices for shift in shifts]).astype(jnp.int32)
        near_sources = jnp.concatenate([sources ^ bits for bits in near])
        held = []
        sent = []
        for payload, _ in outs:
            shards = [payload] + [turned(payload, shift, devices) for shift in shifts[1:]]
            gone = away_maps(others, shards)
            sent.append([crossed(value, bits, devices) for value, bits in zip(gone, near)])
            held += [shard[None] for shard in shards]
        rows = jnp.concatenate([sources * per_dev + i * part for i in range(chunks)])
        maps = write_maps(rows, held, None, shape, part, ordered)
        for i, parts in enumerate(sent):
            maps = write_maps(near_sources * per_dev + i * part, parts, maps, shape, part)
    else:
        collected = lax.all_gather(outs[0][0], "tm", axis=0, tiled=False)
        rows = jnp.arange(devices, dtype=jnp.int32) * per_dev
        maps = write_maps(rows, [collected], None, shape, part, ordered)
    return (flat_pair, maps.transpose(1, 0, 2))


def solution(mesh):
    in_specs = (P(None, ("groups", "tm"), None, None), P("groups"), P(), P(None, None, "tm"))
    out_specs = (P(("groups", "tm"), None, None), P("groups", None, "tm"))
    return jax.shard_map(on_device, mesh=mesh, in_specs=in_specs, out_specs=out_specs, check_vma=False)
```

```python
import functools

import jax
import jax.numpy as jnp
from jax import lax
from jax.experimental import pallas as pl
from jax.experimental.pallas import tpu as pltpu
from jax.sharding import PartitionSpec as P


ITERS = 20
LANES = 128
SUB = 8
PAIR = 16
TURNS = 9
GRANT = pltpu.CompilerParams(vmem_limit_bytes=14 << 20)
MAP_SLOTS = 16
CHUNKS = 2


def lane_order(real, imag, axis):
    ports = real.shape[axis]
    full = ports // LANES * LANES
    tail = ports - full
    half = LANES // 2
    assert 0 < tail <= half
    blank = list(real.shape)
    blank[axis] = half - tail
    blank = jnp.zeros(blank, real.dtype)
    cut = functools.partial(lax.slice_in_dim, axis=axis)
    return jnp.concatenate(
        [cut(real, 0, full), cut(imag, 0, full), cut(real, full, ports), blank, cut(imag, full, ports), blank],
        axis=axis,
    )


def lane_places(ports):
    full = ports // LANES * LANES
    part = jnp.arange(2)[:, None]
    port = jnp.arange(ports)[None, :]
    place = jnp.where(port < full, part * full + port, full + port + part * (LANES // 2))
    return (place[:, :, None] == jnp.arange(2 * full + LANES)).astype(jnp.bfloat16)


def split_lanes(block, full):
    tails = block[:, 2 * full :]
    real = jnp.concatenate([block[:, :full], tails], axis=1)
    imag = jnp.concatenate([block[:, full : 2 * full], pltpu.roll(tails, LANES // 2, 1)], axis=1)
    return real, imag


def power_kernel(
    arr_ref, starts_ref, *refs, ports, group, span
):
    steer_refs, (pay_ref, flat_ref, volt_ref, voltt_ref, scale_ref, lhs_ref, pay_sc) = refs[:-7], refs[-7:]
    _, channels, _, wide = arr_ref.shape
    beams = steer_refs[0].shape[0]
    rows = volt_ref.shape[1] // 2
    full = ports // LANES * LANES
    width = full + LANES
    pad = lhs_ref.shape[1] // 4
    valid = lax.broadcasted_iota(jnp.int32, (beams, width), 1) < ports

    def padded(block):
        if pad == beams:
            return block
        return jnp.concatenate([block, jnp.zeros((pad - beams, width), jnp.float32)], axis=0)

    steer_real, steer_imag = split_lanes(sum(ref[...].astype(jnp.float32) for ref in steer_refs), full)
    steer_real = padded(jnp.where(valid, steer_real, 0.0))
    steer_imag = padded(jnp.where(valid, steer_imag, 0.0))
    energy = steer_real * steer_real + steer_imag * steer_imag
    moment = lax.broadcasted_iota(jnp.int32, (rows, LANES), 0)
    off = jnp.zeros((rows, LANES), jnp.float32)
    for i in range(starts_ref.shape[0]):
        start = starts_ref[i]
        off = jnp.where((moment >= start) & (moment < start + span), 1.0, off)
    on = jnp.concatenate([1.0 - off] * (wide // LANES), axis=1)
    count = jnp.concatenate([jnp.sum(off, axis=0, keepdims=True)] * (width // LANES), axis=1)

    def store_pair(k, both):
        high = both.astype(jnp.bfloat16)
        low = (both - high.astype(jnp.float32)).astype(jnp.bfloat16)
        lhs_ref[k, : 2 * pad] = high
        lhs_ref[k, 2 * pad :] = low

    def halves_dot(k_lhs, rhs):
        out = jnp.dot(k_lhs, rhs, preferred_element_type=jnp.float32)
        return out[: 2 * pad] + out[2 * pad :]

    def prepare(k, carry):
        block = arr_ref[:, pl.ds(k, 1)].astype(jnp.float32).reshape(rows, wide)
        kept = block * on
        gone = block - kept
        power = jnp.sum(gone * gone, axis=0, keepdims=True)
        power_real, power_imag = split_lanes(power, full)
        noise = (power_real + power_imag) / count + 1e-06
        real, imag = split_lanes(kept, full)
        both = jnp.concatenate([real, imag], axis=0)
        volt_ref[k] = both.astype(jnp.bfloat16)
        voltt_ref[k] = both.T.astype(jnp.bfloat16)
        scale_ref[pl.ds(k, 1)] = (1.0 / noise)[None]
        first = energy * (1.0 / jnp.sqrt(noise))
        store_pair(k, jnp.concatenate([first, jnp.zeros_like(first)], axis=0))
        return carry

    lax.fori_loop(0, channels, prepare, 0, unroll=min(4, channels))

    def apply_corr(k):
        part = halves_dot(lhs_ref[k], voltt_ref[k])
        real, imag = part[:pad], part[pad:]
        amp_real = real[:, :rows] + imag[:, rows:]
        amp_imag = imag[:, :rows] - real[:, rows:]
        both = jnp.concatenate(
            [jnp.concatenate([amp_real, -amp_imag], axis=1), jnp.concatenate([amp_imag, amp_real], axis=1)], axis=0
        )
        high = both.astype(jnp.bfloat16)
        low = (both - high.astype(jnp.float32)).astype(jnp.bfloat16)
        out = halves_dot(jnp.concatenate([high, low], axis=0), volt_ref[k])
        real, imag = out[:pad], out[pad:]
        weight = energy * scale_ref[k]
        scaled_real = weight * real
        scaled_imag = weight * imag
        mean = jnp.sum(scaled_real * real + scaled_imag * imag, axis=1, keepdims=True) / (2 * ports)
        factor = lax.rsqrt(mean + 1e-06)
        return real, imag, scaled_real, scaled_imag, factor

    def group_body(g, carry):
        def turn():
            for j in range(group):
                k = g * group + j
                _, _, scaled_real, scaled_imag, factor = apply_corr(k)
                store_pair(k, jnp.concatenate([scaled_real * factor, scaled_imag * factor], axis=0))

        def trip(step, inner):
            for _ in range(TURNS):
                turn()
            return inner

        lax.fori_loop(0, (ITERS - 1) // TURNS, trip, 0)
        for _ in range((ITERS - 1) % TURNS):
            turn()
        for j in range(group):
            k = g * group + j
            real, imag, _, _, factor = apply_corr(k)
            gain = scale_ref[k] * factor
            weight_real = ((steer_real * real - steer_imag * imag) * gain)[:beams]
            weight_imag = ((steer_real * imag + steer_imag * real) * gain)[:beams]
            flat_ref[k, 0] = weight_real[:, :ports].astype(jnp.bfloat16)
            flat_ref[k, 1] = weight_imag[:, :ports].astype(jnp.bfloat16)
            tails = weight_real[:, full:] + pltpu.roll(weight_imag[:, full:], LANES // 2, 1)
            tiles = [weight_real[:, i : i + LANES] for i in range(0, full, LANES)]
            tiles += [weight_imag[:, i : i + LANES] for i in range(0, full, LANES)]
            for i, tile in enumerate(tiles + [tails]):
                pay_sc[i, pl.ds(k, beams, stride=channels)] = tile
        return carry

    lax.fori_loop(0, channels // group, group_body, 0)
    for i in range(pay_sc.shape[0]):
        pay_ref[:, i * LANES : (i + 1) * LANES] = pay_sc[i].astype(jnp.bfloat16)


def here(value):
    return pltpu.with_memory_space_constraint(value, pltpu.VMEM)


def power_weights(arrived, starts, span, steer, ports):
    sources, channels, samples, wide = arrived.shape
    beams = steer[0].shape[0]
    rows = sources * samples
    width = ports // LANES * LANES + LANES
    pad = -(-beams // SUB) * SUB
    group = PAIR
    while channels % group:
        group //= 2
    return pl.pallas_call(
        functools.partial(power_kernel, ports=ports, group=group, span=span),
        out_shape=(
            jax.ShapeDtypeStruct((beams * channels, wide), jnp.bfloat16),
            jax.ShapeDtypeStruct((channels, 2, beams, ports), jnp.bfloat16),
        ),
        in_specs=[
            pl.BlockSpec(memory_space=pltpu.VMEM),
            pl.BlockSpec(memory_space=pltpu.SMEM),
        ]
        + [pl.BlockSpec(memory_space=pltpu.VMEM)] * len(steer),
        out_specs=(pl.BlockSpec(memory_space=pltpu.VMEM), pl.BlockSpec(memory_space=pltpu.VMEM)),
        scratch_shapes=[
            pltpu.VMEM((channels, 2 * rows, width), jnp.bfloat16),
            pltpu.VMEM((channels, width, 2 * rows), jnp.bfloat16),
            pltpu.VMEM((channels, 1, width), jnp.float32),
            pltpu.VMEM((channels, 4 * pad, width), jnp.bfloat16),
            pltpu.VMEM((wide // LANES, beams * channels, LANES), jnp.float32),
        ],
        compiler_params=GRANT,
        name="power",
    )(here(arrived), starts, *steer)


def other_parts(ordered):
    half = LANES // 2
    full = (ordered.shape[0] - LANES) // 2
    real, imag, tails = ordered[:full], ordered[full : 2 * full], ordered[2 * full :]
    return jnp.concatenate([imag, -real, tails[half:], -tails[:half]], axis=0)


def view(rows, ordered):
    pixels = ordered.shape[1]
    taps = jnp.concatenate([ordered, other_parts(ordered)], axis=1)
    response = jnp.dot(rows, taps, preferred_element_type=jnp.float32)
    real, imag = response[:, :pixels], response[:, pixels:]
    return real * real + imag * imag


def away_kernel(*refs, shards, views):
    shard_refs, taps_refs, sent_refs = refs[:shards], refs[shards : shards + views], refs[shards + views :]
    for taps, sent in zip(taps_refs, sent_refs):
        for step, shard in enumerate(shard_refs):
            sent[step] = view(shard[...], taps[...]).astype(jnp.bfloat16)


def away_maps(taps, shards):
    depth, _ = shards[0].shape
    pixels = taps[0].shape[1]
    views = len(taps)
    sent = jax.ShapeDtypeStruct((len(shards), depth, pixels), jnp.bfloat16)
    vmem = pl.BlockSpec(memory_space=pltpu.VMEM)
    return pl.pallas_call(
        functools.partial(away_kernel, shards=len(shards), views=views),
        out_shape=(sent,) * views,
        in_specs=[vmem] * (views + len(shards)),
        out_specs=(vmem,) * views,
        compiler_params=GRANT,
        name="away",
    )(*[here(shard) for shard in shards], *taps)


def write_kernel(rows_ref, *refs, parts, channels, with_taps, begun):
    taps_ref = refs[0] if with_taps else None
    part_refs = refs[with_taps : with_taps + parts]
    out_ref = refs[with_taps + parts + begun]
    buf, sem = refs[-2:]
    pieces = [(part, i) for part in part_refs for i in range(part.shape[0])]
    slots = buf.shape[0]

    def emit(step, slot):
        row = pl.multiple_of(rows_ref[step], channels)
        return pltpu.make_async_copy(buf.at[slot], out_ref.at[:, pl.ds(row, channels)], sem.at[slot])

    def work(piece, slot):
        piece = view(piece, taps_ref[...]) if with_taps else piece.astype(jnp.float32)
        buf[slot] = piece.reshape(buf.shape[1:])

    if slots == len(pieces):
        for step, (part, i) in enumerate(pieces):
            work(part[i], step)
            emit(step, step).start()
        for step in range(slots):
            emit(step, step).wait()
    else:

        def body(step, carry):
            work(part_refs[0][step], 0)
            out = emit(step, 0)
            out.start()
            out.wait()
            return carry

        lax.fori_loop(0, len(pieces), body, 0)


def write_maps(rows, parts, into, shape, channels, taps=None):
    beams, _, pixels = shape
    slots = sum(part.shape[0] for part in parts)
    if slots > MAP_SLOTS:
        assert len(parts) == 1
        slots = 1
    any_space = pl.BlockSpec(memory_space=pl.ANY)
    near = ([] if taps is None else [taps]) + [here(part) if slots > 1 else part for part in parts]
    tails = [] if into is None else [into]
    return pl.pallas_call(
        functools.partial(
            write_kernel,
            parts=len(parts),
            channels=channels,
            with_taps=len(near) - len(parts),
            begun=len(tails),
        ),
        out_shape=jax.ShapeDtypeStruct(shape, jnp.float32),
        in_specs=[pl.BlockSpec(memory_space=pltpu.SMEM)]
        + [pl.BlockSpec(memory_space=pltpu.VMEM)] * len(near)
        + [any_space] * len(tails),
        out_specs=any_space,
        scratch_shapes=[
            pltpu.VMEM((slots, beams, channels, pixels), jnp.float32),
            pltpu.SemaphoreType.DMA((slots,)),
        ],
        input_output_aliases={1 + len(near): 0} if tails else {},
        compiler_params=GRANT,
        name="write",
    )(rows, *near, *tails)


def sum_over(value, devices, lines):
    if devices & (devices - 1):
        return [lax.psum(value, "tm")]
    step = 1
    while step < (4 if lines else devices):
        moved = crossed(value, step, devices)
        value = value + moved
        step *= 2
    if lines:
        moved = [turned(value, shift, devices) for shift in (4, 12, 8)]
        return [value] + moved
    return [value]


def turned(value, shift, count):
    return lax.ppermute(value, "tm", [(i, (i + shift) % count) for i in range(count)])


def crossed(value, bits, count):
    return lax.ppermute(value, "tm", [(i, i ^ bits) for i in range(count)])


def on_device(voltages, off_starts, pointing, patterns):
    devices = lax.axis_size("tm")
    position = lax.axis_index("tm")
    channels, samples_dev, _, ports = voltages.shape
    beams = pointing.shape[0]
    per_dev = channels // devices
    full = ports // LANES * LANES
    total_time = samples_dev * devices
    off_span = max(4, total_time // 32)
    pixels = patterns.shape[2]
    ordered = lane_order(patterns[0], patterns[1], 0)
    pixel_ids = position * pixels + jnp.arange(pixels, dtype=jnp.int32)
    selector = (pointing[:, None] == pixel_ids[None, :]).astype(jnp.bfloat16)
    steer_local = jnp.einsum("bx,lx->bl", selector, ordered, preferred_element_type=jnp.float32)
    lines = devices == 16 and per_dev % (8 * CHUNKS) == 0
    steering = sum_over(steer_local.astype(jnp.bfloat16), devices, lines)

    wide = 2 * full + LANES
    packed = jnp.einsum("ctrp,rpl->ctl", voltages, lane_places(ports), preferred_element_type=jnp.float32)
    blocks = packed.astype(jnp.bfloat16).reshape(devices, per_dev, samples_dev, wide)
    chunks = CHUNKS if lines else 1
    part = per_dev // chunks
    shape = (beams, channels, pixels)

    arrived = []
    for i in range(chunks):
        block = blocks[:, i * part : (i + 1) * part]
        arrived.append(lax.all_to_all(block, "tm", split_axis=0, concat_axis=0, tiled=True))
    near = (2, 3, 1)
    if lines:
        others = [crossed(ordered, bits, devices) for bits in near]

    outs = []
    for block in arrived:
        outs.append(power_weights(block, off_starts, off_span, steering, ports))
    weights = jnp.concatenate([w for _, w in outs], axis=0)
    flat_pair = weights.reshape(per_dev, 2, beams * ports)
    if lines:
        own_rows = []
        held = []
        sent = []

        def send(pieces):
            gone = away_maps(others, [shard for shard, _ in pieces])
            gone = [crossed(value, bits, devices) for value, bits in zip(gone, near)]
            sent.append((gone, [spot for _, spot in pieces]))

        waiting = []
        for i, (payload, _) in enumerate(outs):
            if i + 1 < chunks:
                one, two = crossed(payload, 4, devices), crossed(payload, 8, devices)
                three = crossed(two, 4, devices)
                shards = [payload, one, two, three]
                spots = [(position ^ bits, i * part) for bits in (0, 4, 8, 12)]
                waiting += zip(shards, spots)
            else:
                shards = [payload] + [turned(payload, shift, devices) for shift in (8, 12, 4)]
                spots = [((position - shift) % devices, i * part) for shift in (0, 8, 12, 4)]
                pieces = list(zip(shards, spots))
                send(waiting[:-1] + pieces[:1])
                send(waiting[-1:])
                send(pieces[1:])
            held += [shard[None] for shard in shards]
            own_rows += [source * per_dev + offset for source, offset in spots]

        last = len(sent) - 1
        groups = [[(n, j) for n in range(last) for j in range(3)], [(last, 2), (last, 0)], [(last, 1)]]
        own_rows = jnp.stack(own_rows).astype(jnp.int32)
        near_rows = [
            jnp.stack(
                [(source ^ near[j]) * per_dev + offset for n, j in group for source, offset in sent[n][1]]
            ).astype(jnp.int32)
            for group in groups
        ]
        maps = write_maps(own_rows, held, None, shape, part, ordered)
        for i, group in enumerate(groups):
            maps = write_maps(near_rows[i], [sent[n][0][j] for n, j in group], maps, shape, part)
    else:
        collected = lax.all_gather(outs[0][0], "tm", axis=0, tiled=False)
        rows = jnp.arange(devices, dtype=jnp.int32) * per_dev
        maps = write_maps(rows, [collected], None, shape, part, ordered)
    return (flat_pair, maps.transpose(1, 0, 2))


def solution(mesh):
    in_specs = (P(None, ("groups", "tm"), None, None), P("groups"), P(), P(None, None, "tm"))
    out_specs = (P(("groups", "tm"), None, None), P("groups", None, "tm"))
    return jax.shard_map(on_device, mesh=mesh, in_specs=in_specs, out_specs=out_specs, check_vma=False)
```

```python
import functools

import jax
import jax.numpy as jnp
from jax import lax
from jax.experimental import pallas as pl
from jax.experimental.pallas import tpu as pltpu
from jax.sharding import PartitionSpec as P


ITERS = 20
LANES = 128
SUB = 8
PAIR = 16
TURNS = 9
GRANT = pltpu.CompilerParams(vmem_limit_bytes=14 << 20)
MAP_SLOTS = 16
CHUNKS = 2


def lane_order(real, imag, axis):
    ports = real.shape[axis]
    full = ports // LANES * LANES
    tail = ports - full
    half = LANES // 2
    assert 0 < tail <= half
    blank = list(real.shape)
    blank[axis] = half - tail
    blank = jnp.zeros(blank, real.dtype)
    cut = functools.partial(lax.slice_in_dim, axis=axis)
    return jnp.concatenate(
        [cut(real, 0, full), cut(imag, 0, full), cut(real, full, ports), blank, cut(imag, full, ports), blank],
        axis=axis,
    )


def lane_places(ports):
    full = ports // LANES * LANES
    part = jnp.arange(2)[:, None]
    port = jnp.arange(ports)[None, :]
    place = jnp.where(port < full, part * full + port, full + port + part * (LANES // 2))
    return (place[:, :, None] == jnp.arange(2 * full + LANES)).astype(jnp.bfloat16)


def split_lanes(block, full):
    tails = block[:, 2 * full :]
    real = jnp.concatenate([block[:, :full], tails], axis=1)
    imag = jnp.concatenate([block[:, full : 2 * full], pltpu.roll(tails, LANES // 2, 1)], axis=1)
    return real, imag


def power_kernel(
    arr_ref, starts_ref, *refs, ports, group, span
):
    steer_refs, (pay_ref, flat_ref, volt_ref, voltt_ref, scale_ref, lhs_ref, pay_sc) = refs[:-7], refs[-7:]
    _, channels, _, wide = arr_ref.shape
    beams = steer_refs[0].shape[0]
    rows = volt_ref.shape[1] // 2
    full = ports // LANES * LANES
    width = full + LANES
    pad = lhs_ref.shape[1] // 4
    valid = lax.broadcasted_iota(jnp.int32, (beams, width), 1) < ports

    def padded(block):
        if pad == beams:
            return block
        return jnp.concatenate([block, jnp.zeros((pad - beams, width), jnp.float32)], axis=0)

    steer_real, steer_imag = split_lanes(sum(ref[...].astype(jnp.float32) for ref in steer_refs), full)
    steer_real = padded(jnp.where(valid, steer_real, 0.0))
    steer_imag = padded(jnp.where(valid, steer_imag, 0.0))
    energy = steer_real * steer_real + steer_imag * steer_imag
    moment = lax.broadcasted_iota(jnp.int32, (rows, LANES), 0)
    off = jnp.zeros((rows, LANES), jnp.float32)
    for i in range(starts_ref.shape[0]):
        start = starts_ref[i]
        off = jnp.where((moment >= start) & (moment < start + span), 1.0, off)
    on = jnp.concatenate([1.0 - off] * (wide // LANES), axis=1)
    count = jnp.concatenate([jnp.sum(off, axis=0, keepdims=True)] * (width // LANES), axis=1)

    def store_pair(k, both):
        high = both.astype(jnp.bfloat16)
        low = (both - high.astype(jnp.float32)).astype(jnp.bfloat16)
        lhs_ref[k, : 2 * pad] = high
        lhs_ref[k, 2 * pad :] = low

    def halves_dot(k_lhs, rhs):
        out = jnp.dot(k_lhs, rhs, preferred_element_type=jnp.float32)
        return out[: 2 * pad] + out[2 * pad :]

    def prepare(k, carry):
        block = arr_ref[:, pl.ds(k, 1)].astype(jnp.float32).reshape(rows, wide)
        kept = block * on
        gone = block - kept
        power = jnp.sum(gone * gone, axis=0, keepdims=True)
        power_real, power_imag = split_lanes(power, full)
        noise = (power_real + power_imag) / count + 1e-06
        real, imag = split_lanes(kept, full)
        both = jnp.concatenate([real, imag], axis=0)
        volt_ref[k] = both.astype(jnp.bfloat16)
        voltt_ref[k] = both.T.astype(jnp.bfloat16)
        scale_ref[pl.ds(k, 1)] = (1.0 / noise)[None]
        first = energy * (1.0 / jnp.sqrt(noise))
        store_pair(k, jnp.concatenate([first, jnp.zeros_like(first)], axis=0))
        return carry

    lax.fori_loop(0, channels, prepare, 0, unroll=min(4, channels))

    def apply_corr(k):
        part = halves_dot(lhs_ref[k], voltt_ref[k])
        real, imag = part[:pad], part[pad:]
        amp_real = real[:, :rows] + imag[:, rows:]
        amp_imag = imag[:, :rows] - real[:, rows:]
        both = jnp.concatenate(
            [jnp.concatenate([amp_real, -amp_imag], axis=1), jnp.concatenate([amp_imag, amp_real], axis=1)], axis=0
        )
        high = both.astype(jnp.bfloat16)
        low = (both - high.astype(jnp.float32)).astype(jnp.bfloat16)
        out = halves_dot(jnp.concatenate([high, low], axis=0), volt_ref[k])
        real, imag = out[:pad], out[pad:]
        weight = energy * scale_ref[k]
        scaled_real = weight * real
        scaled_imag = weight * imag
        mean = jnp.sum(scaled_real * real + scaled_imag * imag, axis=1, keepdims=True) / (2 * ports)
        factor = lax.rsqrt(mean + 1e-06)
        return real, imag, scaled_real, scaled_imag, factor

    def group_body(g, carry):
        def turn():
            for j in range(group):
                k = g * group + j
                _, _, scaled_real, scaled_imag, factor = apply_corr(k)
                store_pair(k, jnp.concatenate([scaled_real * factor, scaled_imag * factor], axis=0))

        def trip(step, inner):
            for _ in range(TURNS):
                turn()
            return inner

        lax.fori_loop(0, (ITERS - 1) // TURNS, trip, 0)
        for _ in range((ITERS - 1) % TURNS):
            turn()
        for j in range(group):
            k = g * group + j
            real, imag, _, _, factor = apply_corr(k)
            gain = scale_ref[k] * factor
            weight_real = (steer_real * real - steer_imag * imag) * gain
            weight_imag = (steer_real * imag + steer_imag * real) * gain
            flat_ref[k, 0] = weight_real[:beams, :ports].astype(jnp.bfloat16)
            flat_ref[k, 1] = weight_imag[:beams, :ports].astype(jnp.bfloat16)
            tails = weight_real[:, full:] + pltpu.roll(weight_imag[:, full:], LANES // 2, 1)
            tiles = [weight_real[:, i : i + LANES] for i in range(0, full, LANES)]
            tiles += [weight_imag[:, i : i + LANES] for i in range(0, full, LANES)]
            for i, tile in enumerate(tiles + [tails]):
                pay_sc[i, pl.ds(k, pad, stride=channels)] = tile
        return carry

    lax.fori_loop(0, channels // group, group_body, 0)
    for i in range(pay_sc.shape[0]):
        pay_ref[:, i * LANES : (i + 1) * LANES] = pay_sc[i, : beams * channels].astype(jnp.bfloat16)


def here(value):
    return pltpu.with_memory_space_constraint(value, pltpu.VMEM)


def power_weights(arrived, starts, span, steer, ports):
    sources, channels, samples, wide = arrived.shape
    beams = steer[0].shape[0]
    rows = sources * samples
    width = ports // LANES * LANES + LANES
    pad = -(-beams // SUB) * SUB
    group = PAIR
    while channels % group:
        group //= 2
    return pl.pallas_call(
        functools.partial(power_kernel, ports=ports, group=group, span=span),
        out_shape=(
            jax.ShapeDtypeStruct((beams * channels, wide), jnp.bfloat16),
            jax.ShapeDtypeStruct((channels, 2, beams, ports), jnp.bfloat16),
        ),
        in_specs=[
            pl.BlockSpec(memory_space=pltpu.VMEM),
            pl.BlockSpec(memory_space=pltpu.SMEM),
        ]
        + [pl.BlockSpec(memory_space=pltpu.VMEM)] * len(steer),
        out_specs=(pl.BlockSpec(memory_space=pltpu.VMEM), pl.BlockSpec(memory_space=pltpu.VMEM)),
        scratch_shapes=[
            pltpu.VMEM((channels, 2 * rows, width), jnp.bfloat16),
            pltpu.VMEM((channels, width, 2 * rows), jnp.bfloat16),
            pltpu.VMEM((channels, 1, width), jnp.float32),
            pltpu.VMEM((channels, 4 * pad, width), jnp.bfloat16),
            pltpu.VMEM((wide // LANES, pad * channels, LANES), jnp.float32),
        ],
        compiler_params=GRANT,
        name="power",
    )(here(arrived), starts, *steer)


def other_parts(ordered):
    half = LANES // 2
    full = (ordered.shape[0] - LANES) // 2
    real, imag, tails = ordered[:full], ordered[full : 2 * full], ordered[2 * full :]
    return jnp.concatenate([imag, -real, tails[half:], -tails[:half]], axis=0)


def view(rows, ordered):
    pixels = ordered.shape[1]
    taps = jnp.concatenate([ordered, other_parts(ordered)], axis=1)
    response = jnp.dot(rows, taps, preferred_element_type=jnp.float32)
    real, imag = response[:, :pixels], response[:, pixels:]
    return real * real + imag * imag


def away_kernel(*refs, shards, views):
    shard_refs, taps_refs, sent_refs = refs[:shards], refs[shards : shards + views], refs[shards + views :]
    for taps, sent in zip(taps_refs, sent_refs):
        for step, shard in enumerate(shard_refs):
            sent[step] = view(shard[...], taps[...]).astype(jnp.bfloat16)


def away_maps(taps, shards):
    depth, _ = shards[0].shape
    pixels = taps[0].shape[1]
    views = len(taps)
    sent = jax.ShapeDtypeStruct((len(shards), depth, pixels), jnp.bfloat16)
    vmem = pl.BlockSpec(memory_space=pltpu.VMEM)
    return pl.pallas_call(
        functools.partial(away_kernel, shards=len(shards), views=views),
        out_shape=(sent,) * views,
        in_specs=[vmem] * (views + len(shards)),
        out_specs=(vmem,) * views,
        compiler_params=GRANT,
        name="away",
    )(*[here(shard) for shard in shards], *taps)


def write_kernel(rows_ref, *refs, parts, channels, with_taps, begun):
    taps_ref = refs[0] if with_taps else None
    part_refs = refs[with_taps : with_taps + parts]
    out_ref = refs[with_taps + parts + begun]
    buf, sem = refs[-2:]
    pieces = [(part, i) for part in part_refs for i in range(part.shape[0])]
    slots = buf.shape[0]

    def emit(step, slot):
        row = pl.multiple_of(rows_ref[step], channels)
        return pltpu.make_async_copy(buf.at[slot], out_ref.at[:, pl.ds(row, channels)], sem.at[slot])

    def work(piece, slot):
        piece = view(piece, taps_ref[...]) if with_taps else piece.astype(jnp.float32)
        buf[slot] = piece.reshape(buf.shape[1:])

    if slots == len(pieces):
        for step, (part, i) in enumerate(pieces):
            work(part[i], step)
            emit(step, step).start()
        for step in range(slots):
            emit(step, step).wait()
    else:

        def body(step, carry):
            work(part_refs[0][step], 0)
            out = emit(step, 0)
            out.start()
            out.wait()
            return carry

        lax.fori_loop(0, len(pieces), body, 0)


def write_maps(rows, parts, into, shape, channels, taps=None):
    beams, _, pixels = shape
    slots = sum(part.shape[0] for part in parts)
    if slots > MAP_SLOTS:
        assert len(parts) == 1
        slots = 1
    any_space = pl.BlockSpec(memory_space=pl.ANY)
    near = ([] if taps is None else [taps]) + [here(part) if slots > 1 else part for part in parts]
    tails = [] if into is None else [into]
    return pl.pallas_call(
        functools.partial(
            write_kernel,
            parts=len(parts),
            channels=channels,
            with_taps=len(near) - len(parts),
            begun=len(tails),
        ),
        out_shape=jax.ShapeDtypeStruct(shape, jnp.float32),
        in_specs=[pl.BlockSpec(memory_space=pltpu.SMEM)]
        + [pl.BlockSpec(memory_space=pltpu.VMEM)] * len(near)
        + [any_space] * len(tails),
        out_specs=any_space,
        scratch_shapes=[
            pltpu.VMEM((slots, beams, channels, pixels), jnp.float32),
            pltpu.SemaphoreType.DMA((slots,)),
        ],
        input_output_aliases={1 + len(near): 0} if tails else {},
        compiler_params=GRANT,
        name="write",
    )(rows, *near, *tails)


def sum_over(value, devices, lines):
    if devices & (devices - 1):
        return [lax.psum(value, "tm")]
    step = 1
    while step < (4 if lines else devices):
        moved = crossed(value, step, devices)
        value = value + moved
        step *= 2
    if lines:
        moved = [turned(value, shift, devices) for shift in (4, 12, 8)]
        return [value] + moved
    return [value]


def turned(value, shift, count):
    return lax.ppermute(value, "tm", [(i, (i + shift) % count) for i in range(count)])


def crossed(value, bits, count):
    return lax.ppermute(value, "tm", [(i, i ^ bits) for i in range(count)])


def on_device(voltages, off_starts, pointing, patterns):
    devices = lax.axis_size("tm")
    position = lax.axis_index("tm")
    channels, samples_dev, _, ports = voltages.shape
    beams = pointing.shape[0]
    per_dev = channels // devices
    full = ports // LANES * LANES
    total_time = samples_dev * devices
    off_span = max(4, total_time // 32)
    pixels = patterns.shape[2]
    ordered = lane_order(patterns[0], patterns[1], 0)
    pixel_ids = position * pixels + jnp.arange(pixels, dtype=jnp.int32)
    selector = (pointing[:, None] == pixel_ids[None, :]).astype(jnp.bfloat16)
    steer_local = jnp.einsum("bx,lx->bl", selector, ordered, preferred_element_type=jnp.float32)
    lines = devices == 16 and per_dev % (8 * CHUNKS) == 0
    steering = sum_over(steer_local.astype(jnp.bfloat16), devices, lines)

    wide = 2 * full + LANES
    packed = jnp.einsum("ctrp,rpl->ctl", voltages, lane_places(ports), preferred_element_type=jnp.float32)
    blocks = packed.astype(jnp.bfloat16).reshape(devices, per_dev, samples_dev, wide)
    chunks = CHUNKS if lines else 1
    part = per_dev // chunks
    shape = (beams, channels, pixels)

    arrived = []
    for i in range(chunks):
        if i:
            blocks, steering[0] = lax.optimization_barrier((blocks, steering[0]))
        block = blocks[:, i * part : (i + 1) * part]
        arrived.append(lax.all_to_all(block, "tm", split_axis=0, concat_axis=0, tiled=True))
    near = (2, 3, 1)
    if lines:
        others = [crossed(ordered, bits, devices) for bits in near]

    outs = []
    for block in arrived:
        outs.append(power_weights(block, off_starts, off_span, steering, ports))
    weights = jnp.concatenate([w for _, w in outs], axis=0)
    flat_pair = weights.reshape(per_dev, 2, beams * ports)
    if lines:
        own_rows = []
        held = []
        sent = []

        def send(pieces):
            gone = away_maps(others, [shard for shard, _ in pieces])
            gone = [crossed(value, bits, devices) for value, bits in zip(gone, near)]
            sent.append((gone, [spot for _, spot in pieces]))

        waiting = []
        for i, (payload, _) in enumerate(outs):
            if i + 1 < chunks:
                one, two = crossed(payload, 4, devices), crossed(payload, 8, devices)
                three = crossed(two, 4, devices)
                shards = [payload, one, two, three]
                spots = [(position ^ bits, i * part) for bits in (0, 4, 8, 12)]
                waiting += zip(shards, spots)
            else:
                shards = [payload] + [turned(payload, shift, devices) for shift in (8, 12, 4)]
                spots = [((position - shift) % devices, i * part) for shift in (0, 8, 12, 4)]
                pieces = list(zip(shards, spots))
                send(waiting[:-1] + pieces[:1])
                send(waiting[-1:])
                send(pieces[1:])
            held += [shard[None] for shard in shards]
            own_rows += [source * per_dev + offset for source, offset in spots]

        last = len(sent) - 1
        groups = [[(n, j) for n in range(last) for j in range(3)], [(last, 2), (last, 0)], [(last, 1)]]
        own_rows = jnp.stack(own_rows).astype(jnp.int32)
        near_rows = [
            jnp.stack(
                [(source ^ near[j]) * per_dev + offset for n, j in group for source, offset in sent[n][1]]
            ).astype(jnp.int32)
            for group in groups
        ]
        maps = write_maps(own_rows, held, None, shape, part, ordered)
        for i, group in enumerate(groups):
            maps = write_maps(near_rows[i], [sent[n][0][j] for n, j in group], maps, shape, part)
    else:
        collected = lax.all_gather(outs[0][0], "tm", axis=0, tiled=False)
        rows = jnp.arange(devices, dtype=jnp.int32) * per_dev
        maps = write_maps(rows, [collected], None, shape, part, ordered)
    return (flat_pair, maps.transpose(1, 0, 2))


def solution(mesh):
    in_specs = (P(None, ("groups", "tm"), None, None), P("groups"), P(), P(None, None, "tm"))
    out_specs = (P(("groups", "tm"), None, None), P("groups", None, "tm"))
    return jax.shard_map(on_device, mesh=mesh, in_specs=in_specs, out_specs=out_specs, check_vma=False)
```
